512 devices in a mesh: mem: 8 (over z), var: 64 (over y, x, core).
Axes of the slice: x: 4, y: 8, z: 8, core: 2. Of those that a mesh axis runs over, the one named last changes fastest.
Arguments:
- ensemble: float32 [80, 524288], P('mem', 'var'), may hold values from -6 to 6
- owner: int32 [4, 512, 1], replicated, may hold values from 0 to 511; in each aligned block of 512 rows (0 to 511, 512 to 1023, ..., all dimensions but the last counted through in order) at most 8 rows name the same one
- slot: int32 [4, 512], replicated, may hold values from 0 to 1023
- pattern: int32 [4, 2048, 2], P(None, 'var'), may hold values from 0 to 4, as said below
- loc_weight: float32 [4, 2048, 2], P(None, 'var'), may hold values from 0.02 to 0.2
- obs_value: float32 [4, 512], replicated, may hold values from -6 to 6
- obs_errvar: float32 [4, 512], replicated, may hold values from 0.25 to 4
- batch_order: int32 [4], replicated, may hold values from 0 to 3, each once
Outputs:
- analysis: float32 [80, 524288], P('mem', 'var')
The draws below stay inside these ranges and needn't reach their ends.
Inputs may be any that keep to these rules, and one draw needn't show every extreme that they name: `owner`: in each batch no device block owns more than 8 observations, and in some batch some device block owns exactly 8. `pattern`: each row lists one to 2 different observation blocks first and 4 in its unused entries; the first row of every batch lists 2 blocks. `batch_order`: each batch appears once.
All inputs are finite; a program needn't handle non-finite values.
Results may differ from the reference program's by a relative error of at most 0.0001.
Values sent between devices are 32-bit elements; how exact they have to be, the bound alone decides.
No kernel may reach another device: no remote copies, remote signals or barrier semaphores. Data moves between devices by JAX's collectives and lax.ppermute only.
A program may use at most 64 MiB of HBM per device.

```python
import math
import jax
import jax.numpy as jnp
import numpy as np
from jax import lax

M = 80
VD = 1024
VBLK = 256
NOBS = 512
OBLK = 128
PAD = 2
NB = 4
NOB = 4
CAP = 8
NV = 524288
NVB = 2048
DEVICES = 512


def draw_pattern(key, part):
    first_key, second_key = jax.random.split(jax.random.fold_in(key, 17))
    scores = jax.random.randint(first_key, (NB, NVB, NOB), 0, 1 << 20) * NOB + jnp.arange(NOB, dtype=jnp.int32)
    ordered = jnp.argsort(scores, axis=-1, stable=True)[..., :PAD].astype(jnp.int32)
    counts = jax.random.randint(second_key, (NB, NVB, 1), 1, PAD + 1).astype(jnp.int32)
    counts = counts.at[:, 0, :].set(PAD)
    used = jnp.arange(PAD, dtype=jnp.int32)[None, None, :] < counts
    return jnp.where(used, ordered, NOB).astype(jnp.int32)


def plant(drawn, stream_key, least, largest):
    longest = drawn.shape.index(max(drawn.shape))
    spots = []
    for shift in (0, 1):
        where = [jax.random.randint(jax.random.fold_in(stream_key, axis), (), 0, length) for axis, length in enumerate(drawn.shape)]
        where[longest] = (where[longest] + shift) % drawn.shape[longest]
        spots.append(tuple(where))
    return drawn.at[spots[0]].set(least).at[spots[1]].set(largest)


def block_levels(stream_key, extent, pieces, smallest, largest):
    factor_of, own = 1.0, jax.random.fold_in(stream_key, 6)
    for position, parts in pieces:
        steps = jnp.exp(jax.random.uniform(jax.random.fold_in(own, position), (parts,), jnp.float32, smallest / len(pieces), largest / len(pieces)))
        factor_of = factor_of * jnp.repeat(steps, extent[position] // parts).reshape([-1 if axis == position else 1 for axis in range(len(extent))])
    return factor_of


def deal_out(rng, own, number, rows, count, top, bound, skew):
    sequence = jax.random.permutation(rng, count)
    packed, ordinary = portions_of(count, rows * top, bound, skew, True), portions_of(count, rows * top, bound, skew, False)
    places = jnp.arange(count)

    def named(lengths, rotation):
        used = int((lengths > 0).sum())
        fixed = max(1, used // 4)
        shifted = fixed + (places - fixed + rotation * (used - fixed)) % max(1, count - fixed)
        return jnp.zeros((count,), jnp.int32).at[sequence[jnp.where(places < fixed, places, shifted)]].set(jnp.asarray(lengths, jnp.int32))

    lengths = jnp.where(number % 4 == 0, named(packed, number // 4), named(ordinary, number - number // 4 - 1))
    mixed = jax.random.permutation(jax.random.fold_in(own, 3), count)
    giver, receiver = mixed[0:count // 2 * 2:2], mixed[1:count // 2 * 2:2]
    room = jnp.minimum(lengths[giver] - 1, bound - lengths[receiver]) // 2
    room = jnp.where((giver == sequence[0]) | (receiver == sequence[0]) | (lengths[receiver] == 0), 0, jnp.maximum(room, 0))
    shifted = jax.random.randint(jax.random.fold_in(own, 4), (count // 2,), 0, 1 << 20) % (room + 1)
    lengths = lengths.at[giver].add(-shifted).at[receiver].add(shifted)
    items = jnp.searchsorted(jnp.cumsum(lengths), jnp.arange(rows * top), side="right").astype(jnp.int32)
    listing = items.reshape(top, rows).T
    listing = listing[jax.random.permutation(jax.random.fold_in(own, 1), rows)]
    rotation = jax.random.randint(jax.random.fold_in(own, 2), (rows, 1), 0, top)
    return jnp.take_along_axis(listing, (jnp.arange(top)[None, :] + rotation) % top, axis=1)


def portions_of(number_of, total, most, slope, full):
    weights = [(1 << 20) // math.isqrt(standing ** slope) + 1 for standing in range(1, number_of + 1)]
    largest = most if full else min(most, max(-(-total // number_of), total * weights[0] // sum(weights)))
    least = 1 if total - largest >= number_of - 1 else 0
    holding, rest = [largest] + [least] * (number_of - 1), total - largest - least * (number_of - 1)
    while rest > 0:
        candidates = [i for i in range(1, number_of) if holding[i] < largest] or [i for i in range(1, number_of) if holding[i] < most]
        pool, budget = sum([weights[i] for i in candidates]), rest
        for i in candidates:
            more = min(most - holding[i], max(1, budget * weights[i] // pool), rest)
            holding[i] = holding[i] + more
            rest = rest - more
    return np.array(holding)


def scatter_about(own_key, dims, width, bound, pieces=(), held_as=jnp.bfloat16):
    gain = block_levels(own_key, dims, pieces, -0.22, 0.18) if pieces else 1.0
    array = jax.random.normal(own_key, dims, jnp.float32) * width * gain
    return jnp.minimum(jnp.maximum(array, -bound), bound).astype(held_as)


def setup_inputs(seed: int = 0) -> dict:
    splits = jax.random.split(jax.random.key(seed), 9)
    ensemble = scatter_about(splits[0], (M, NV), 1.0, 6.0, ((0, 8), (1, 64)), jnp.float32)
    owner_keys = jax.random.split(jax.random.fold_in(splits[1], 1), NB * NOBS // NOBS)
    owner_turns = jax.random.permutation(jax.random.fold_in(splits[1], 3), NB * NOBS // NOBS)
    owner = jax.vmap(lambda own, number: deal_out(jax.random.fold_in(splits[1], 2), own, number, NOBS, DEVICES, 1, CAP, 2))(owner_keys, owner_turns).reshape((NB, NOBS, 1))
    slot = plant(jax.random.randint(splits[2], (NB, NOBS), 0, VD), jax.random.fold_in(splits[2], 1), 0, VD - 1).astype(jnp.int32)
    pattern = draw_pattern(jax.random.fold_in(splits[8], 71), 0)
    loc_weight = jnp.clip(jnp.exp(math.log(0.2) - 2.3025851 * jax.random.uniform(splits[4], (NB, NVB, PAD), jnp.float32) ** block_levels(splits[4], (NB, NVB, PAD), ((1, 64),), -0.2, 0.2)), 0.02, 0.2)
    obs_value = scatter_about(splits[5], (NB, NOBS), 1.0, 6.0, (), jnp.float32)
    obs_errvar = jnp.clip(jnp.exp(jax.random.uniform(splits[6], (NB, NOBS), jnp.float32, math.log(0.25), math.log(4.0))), 0.25, 4.0)
    batch_order = jax.random.permutation(splits[7], NB).astype(jnp.int32)
    return dict(ensemble=ensemble, owner=owner, slot=slot, pattern=pattern, loc_weight=loc_weight, obs_value=obs_value, obs_errvar=obs_errvar, batch_order=batch_order)


exact_prec = lax.Precision.HIGHEST

def observe(prior_obs, value_obs, errvar_obs):
    members = prior_obs.shape[0]
    center = lax.optimization_barrier(jnp.mean(prior_obs, axis=0))
    deviate = prior_obs - center
    spread = lax.optimization_barrier(jnp.sum(deviate * deviate, axis=0)) / (members - 1)
    total_var = spread + errvar_obs
    posterior = (center * errvar_obs + value_obs * spread) / total_var
    factor = jnp.sqrt(errvar_obs / total_var)
    increment = posterior - center + (factor - 1.0) * deviate
    gain_obs = deviate / ((members - 1) * (spread + 1e-06))
    return (increment, gain_obs)

def with_blank(values_in, obs_blocks):
    members = values_in.shape[0]
    shaped = values_in.reshape(members, obs_blocks, OBLK)
    return jnp.concatenate([shaped, jnp.zeros_like(shaped[:, :1])], axis=1)

def reference(ensemble, owner, slot, pattern, loc_weight, obs_value, obs_errvar, batch_order):
    current = ensemble
    for stepnum in range(NB):
        batch_now = batch_order[stepnum]
        column = (owner[batch_now, :, 0] * VD + slot[batch_now]).astype(jnp.int32)
        prior_obs = jnp.take(current, column, axis=1)
        increment, gain_obs = observe(prior_obs, obs_value[batch_now], obs_errvar[batch_now])
        incr_blocks = with_blank(increment, NOB)
        gain_blocks = with_blank(gain_obs, NOB)
        blocks = jnp.transpose(current.reshape(M, NVB, VBLK), (1, 0, 2))

        def update(entries):
            var_block, pattern_row, weight_row = entries
            incr_sel = jnp.take(incr_blocks, pattern_row, axis=1)
            gain_sel = jnp.take(gain_blocks, pattern_row, axis=1) * weight_row[None, :, None]
            mixing = jnp.einsum('mpk,npk->mn', incr_sel, gain_sel, precision=exact_prec)
            deviation = var_block - lax.optimization_barrier(jnp.mean(var_block, axis=0))
            return var_block + jnp.dot(mixing, deviation, precision=exact_prec)
        blocks = lax.map(update, (blocks, pattern[batch_now], loc_weight[batch_now]))
        current = jnp.transpose(blocks, (1, 0, 2)).reshape(M, NV)
    return current
```

```python
import jax
import jax.numpy as jnp
from jax import lax
from jax.experimental import pallas as pl
from jax.experimental.pallas import tpu as pltpu
from jax.sharding import Mesh, PartitionSpec as P

M, NOBS, NB = 80, 512, 4
NZ, NY, NX, NC = 8, 8, 4, 2
MZ = M // NZ
WIDTH = 8192
VBLK = 256
NBLK = WIDTH // VBLK
OBLK = 128
GROUPS = NB * NOBS // OBLK
LANE = 128
K3 = 3 * M
F32, BF16 = jnp.float32, jnp.bfloat16


def halves(x):
    high = x.astype(BF16)
    return high, (x - high.astype(F32)).astype(BF16)


def high_high_low(x, lanes):
    high = x.astype(BF16).astype(F32)
    return jnp.where(lanes < 2 * M, high, x - high)


def extract_kernel(order, pay, owner, slot, pattern, weight, out, table):
    z = lax.axis_index("z")
    var = (lax.axis_index("y") * NX + lax.axis_index("x")) * NC + lax.axis_index("c")
    q = order[z // 2]
    first = (z % 2) * 2
    table[...] = jnp.zeros_like(table)
    names, sizes = pattern[q], weight[q]
    for j in range(2):
        hit = jnp.where(names == first + j, sizes, 0.0)
        table[j : j + 1, 0:NBLK] = jnp.sum(hit, axis=0, keepdims=True)
    weights = table[...]
    quarter = lax.broadcasted_iota(jnp.int32, (8, LANE), 0) % 4
    zeros = jnp.zeros((4, LANE), F32)
    for t in range(NB):
        batch = order[t]
        owners = owner[pl.ds(batch, 1), :]
        slots = slot[pl.ds(batch, 1), :]
        for p in range(4):
            g = 4 * t + p
            own = owners[:, p * OBLK : (p + 1) * OBLK]
            col = (own & 7) * 1024 + slots[:, p * OBLK : (p + 1) * OBLK]
            mine = (own >> 3) == var
            tile = jnp.broadcast_to(jnp.where(mine, col >> 7, -1), (8, LANE))
            lane = jnp.broadcast_to(col & 127, (8, LANE))
            low = jnp.zeros((8, LANE), F32)
            for j in range(64):
                got = jnp.take_along_axis(
                    pay[:, j * LANE : (j + 1) * LANE], lane, axis=1, mode="promise_in_bounds"
                )
                low = jnp.where(tile == j, got, low)
            rest = jnp.zeros((8, LANE), F32)
            shifted = tile - quarter * 16
            for j in range(16):
                got = jnp.take_along_axis(
                    pay[:, WIDTH + j * LANE : WIDTH + (j + 1) * LANE], lane, axis=1, mode="promise_in_bounds"
                )
                rest = jnp.where((shifted == j) & (tile >= 0), got, rest)
            block = jnp.where(mine, col >> 8, LANE - 1)
            local = jnp.take_along_axis(
                weights, jnp.broadcast_to(block, (8, LANE)), axis=1, mode="promise_in_bounds"
            )
            c, y = g // 8, g % 8
            base = y * NX * NC + c
            out[base] = low[0:4]
            out[base + NC] = low[4:8]
            out[base + 2 * NC, 0:1] = jnp.sum(rest[0:4], axis=0, keepdims=True)
            out[base + 2 * NC, 1:2] = jnp.sum(rest[4:8], axis=0, keepdims=True)
            out[base + 2 * NC, 2:4] = local[0:2]
            out[base + 3 * NC] = zeros


def filter_kernel(
    order, own_half, other_half, value, errvar, pattern, weight, ens, gathered, out,
    obs, local, t3, tv, table, dscr, state, rest, sems,
):
    loads = [pltpu.make_async_copy(gathered.at[:, 0:WIDTH], state, sems.at[16])]
    for j in range(16):
        at = WIDTH + j * LANE
        loads.append(pltpu.make_async_copy(gathered.at[:, at : at + LANE], rest.at[j], sems.at[j]))
    for load in loads:
        load.start()
    z = lax.axis_index("z")
    first_core = lax.axis_index("c") == 0

    for g in range(GROUPS):
        c, y = g // 8, g % 8
        cols = slice(g * LANE, (g + 1) * LANE)

        def piece(x, zz):
            a, b = own_half[x, zz, y], other_half[x, zz, y]
            return jnp.where(first_core, a, b) if c == 0 else jnp.where(first_core, b, a)

        for zz in range(NZ):
            obs[zz * 8 : zz * 8 + 4, cols] = piece(0, zz)
            obs[zz * 8 + 4 : zz * 8 + 8, cols] = piece(1, zz)
            last = piece(2, zz)
            obs[64 + zz * 2 : 66 + zz * 2, cols] = last[0:2]
            local[zz * 2 : zz * 2 + 2, cols] = last[2:4]

    table[...] = jnp.zeros_like(table)
    for s in range(NB):
        names, sizes = pattern[order[s]], weight[order[s]]
        for p in range(4):
            hit = jnp.where(names == p, sizes, 0.0)
            table[4 * s + p : 4 * s + p + 1, 0:NBLK] = jnp.sum(hit, axis=0, keepdims=True)
    by_block = jnp.transpose(table[...])

    lanes = lax.broadcasted_iota(jnp.int32, (M, K3), 1)
    for t in range(NB):
        batch = order[t]
        val = value[pl.ds(batch, 1), :]
        err = errvar[pl.ds(batch, 1), :]
        prior = obs[:, t * NOBS : (t + 1) * NOBS]
        center = jnp.sum(prior, axis=0, keepdims=True) * (1.0 / M)
        pert = prior - center
        spread = jnp.sum(pert * pert, axis=0, keepdims=True) * (1.0 / (M - 1))
        total = spread + err
        posterior = (center * err + val * spread) / total
        factor = jnp.sqrt(err / total)
        increment = (posterior - center) + (factor - 1.0) * pert
        gain = pert * (1.0 / ((M - 1) * (spread + 1e-6)))
        gain = gain - jnp.sum(gain, axis=0, keepdims=True) * (1.0 / M)
        ih, il = halves(increment)
        gh, gl = halves(gain)
        for p in range(4):
            s = slice(p * OBLK, (p + 1) * OBLK)
            left = jnp.concatenate([ih[:, s], ih[:, s], il[:, s]], axis=1)
            right = jnp.concatenate([gh[:, s], gl[:, s], gh[:, s]], axis=1)
            right = jnp.concatenate([right, right, right], axis=0)
            mix = lax.dot_general(left, right, (((1,), (1,)), ((), ())), preferred_element_type=F32)
            t3[p * M : (p + 1) * M, :] = high_high_low(mix, lanes).astype(BF16)
            mh, ml = halves(mix)
            tv[4 * t + p] = jnp.concatenate([mh, ml, mh], axis=0)
        if t < NB - 1:
            mixing = t3[...]
            for n in range((t + 1) * NOBS, NB * NOBS, 256):
                x = obs[:, n : n + 256]
                xh, xl = halves(x)
                got = jnp.dot(mixing, jnp.concatenate([xh, xl, xh], axis=0), preferred_element_type=F32)
                for p in range(4):
                    x = x + local[4 * t + p : 4 * t + p + 1, n : n + 256] * got[p * M : (p + 1) * M]
                obs[:, n : n + 256] = x

    rows = MZ * NBLK
    lane = lax.broadcasted_iota(jnp.int32, (rows, K3), 1)
    within = lane - jnp.where(lane >= 2 * M, 2 * M, jnp.where(lane >= M, M, 0))
    member = lax.broadcasted_iota(jnp.int32, (rows, K3), 0) // NBLK
    place = jnp.where(member < 8, z * 8 + member, 64 + z * 2 + member - 8)
    unit = (within == place).astype(F32)
    delta = jnp.zeros((rows, K3), F32)
    for s in reversed(range(NB)):
        left = high_high_low(unit + delta, lane).astype(BF16)
        for p in range(4):
            got = jnp.dot(left, tv[4 * s + p], preferred_element_type=F32)
            w = jnp.broadcast_to(by_block[0:NBLK, 4 * s + p : 4 * s + p + 1], (NBLK, K3))
            delta = delta + jnp.concatenate([w] * MZ, axis=0) * got
    delta = high_high_low(delta, lane)
    dscr[0] = delta[:, 0:LANE]
    dscr[1, :, 0 : K3 - LANE] = delta[:, LANE:K3]

    for load in loads:
        load.wait()
    for b in range(NBLK):
        cols = slice(b * VBLK, (b + 1) * VBLK)
        q, r = b // 8, b % 8
        tail = [rest[2 * r + i, pl.ds(q, 16, stride=4), :] for i in range(2)]
        x = jnp.concatenate([state[:, cols], jnp.concatenate(tail, axis=1)], axis=0)
        xh, xl = halves(x)
        left = [dscr[i, pl.ds(b, MZ, stride=NBLK), :] for i in range(2)]
        left = jnp.concatenate(left, axis=1)[:, 0:K3].astype(BF16)
        got = jnp.dot(left, jnp.concatenate([xh, xl, xh], axis=0), preferred_element_type=F32)
        out[:, cols] = ens[:, cols] + got


def per_device(ensemble, owner, slot, pattern, loc_weight, obs_value, obs_errvar, batch_order):
    vmem = pl.BlockSpec(memory_space=pltpu.VMEM)
    smem = pl.BlockSpec(memory_space=pltpu.SMEM)
    pay = jnp.concatenate([ensemble[:8], ensemble[8:].reshape(8, WIDTH // 4)], axis=1)
    gathered = lax.all_gather(pay, "z", axis=0, tiled=True)
    names = jnp.transpose(pattern, (0, 2, 1))
    sizes = jnp.transpose(loc_weight, (0, 2, 1))
    placed = pl.pallas_call(
        extract_kernel,
        out_shape=jax.ShapeDtypeStruct((NY * NX * NC, 4, LANE), F32),
        in_specs=[smem, vmem, vmem, vmem, vmem, vmem],
        out_specs=vmem,
        scratch_shapes=[pltpu.VMEM((8, LANE), F32)],
    )(batch_order, pay, owner[:, :, 0], slot, names, sizes)
    parts = lax.all_to_all(placed, ("y", "x", "c"), split_axis=0, concat_axis=0, tiled=True)
    mine = jnp.sum(parts, axis=0, keepdims=True)
    mine = jnp.broadcast_to(mine, (NZ * NY, 4, LANE))
    plane = lax.all_to_all(mine, ("z", "y"), split_axis=0, concat_axis=0, tiled=True)
    plane = jnp.broadcast_to(plane[None], (NX, NZ * NY, 4, LANE))
    half = lax.all_to_all(plane, "x", split_axis=0, concat_axis=0, tiled=True)
    half = half.reshape(NX, NZ, NY, 4, LANE)
    other = lax.ppermute(half, "c", [(0, 1), (1, 0)])
    return pl.pallas_call(
        filter_kernel,
        out_shape=jax.ShapeDtypeStruct((MZ, WIDTH), F32),
        in_specs=[smem] + [vmem] * 7 + [pl.BlockSpec(memory_space=pl.ANY)],
        out_specs=vmem,
        scratch_shapes=[
            pltpu.VMEM((M, NB * NOBS), F32),
            pltpu.VMEM((16, NB * NOBS), F32),
            pltpu.VMEM((4 * M, K3), BF16),
            pltpu.VMEM((16, K3, K3), BF16),
            pltpu.VMEM((LANE, LANE), F32),
            pltpu.VMEM((2, MZ * NBLK, LANE), F32),
            pltpu.VMEM((NZ * 8, WIDTH), F32),
            pltpu.VMEM((16, NZ * 8, LANE), F32),
            pltpu.SemaphoreType.DMA((17,)),
        ],
        compiler_params=pltpu.CompilerParams(vmem_limit_bytes=40 << 20),
    )(batch_order, half, other, obs_value, obs_errvar, names, sizes, ensemble, gathered)


def solution(mesh):
    fine = Mesh(mesh.devices.reshape(NZ, NY, NX, NC), ("z", "y", "x", "c"))
    var = ("y", "x", "c")
    in_specs = (P("z", var), P(), P(), P(None, var, None), P(None, var, None), P(), P(), P())
    return jax.shard_map(
        per_device, mesh=fine, in_specs=in_specs, out_specs=P("z", var), check_vma=False
    )
```

```python
import jax
import jax.numpy as jnp
from jax import lax
from jax.experimental import pallas as pl
from jax.experimental.pallas import tpu as pltpu
from jax.sharding import Mesh, PartitionSpec as P

M, NOBS, NB = 80, 512, 4
NZ, NY, NX, NC = 8, 8, 4, 2
MZ = M // NZ
WIDTH = 8192
VBLK = 256
NBLK = WIDTH // VBLK
OBLK = 128
GROUPS = NB * NOBS // OBLK
LANE = 128
K3 = 3 * M
F32, BF16 = jnp.float32, jnp.bfloat16


def halves(x):
    high = x.astype(BF16)
    return high, (x - high.astype(F32)).astype(BF16)


def high_high_low(x, lanes):
    high = x.astype(BF16).astype(F32)
    return jnp.where(lanes < 2 * M, high, x - high)


def extract_kernel(order, ens, owner, slot, pattern, weight, out, pay, table):
    z = lax.axis_index("z")
    var = (lax.axis_index("y") * NX + lax.axis_index("x")) * NC + lax.axis_index("c")
    pay[:, 0:WIDTH] = ens[0:8, :]
    for m in range(2):
        for quarter in range(4):
            row = 2 * quarter + m
            at = quarter * (WIDTH // 4)
            pay[row : row + 1, WIDTH:] = ens[8 + m : 9 + m, at : at + WIDTH // 4]
    q = order[z // 2]
    first = (z % 2) * 2
    table[...] = jnp.zeros_like(table)
    names, sizes = pattern[q], weight[q]
    for j in range(2):
        hit = jnp.where(names == first + j, sizes, 0.0)
        table[j : j + 1, 0:NBLK] = jnp.sum(hit, axis=0, keepdims=True)
    weights = table[...]
    row = lax.broadcasted_iota(jnp.int32, (8, LANE), 0)
    quarter = row >> 1
    for t in range(NB):
        batch = order[t]
        owners = owner[batch]
        slots = slot[pl.ds(batch, 1), :]
        for p in range(4):
            g = 4 * t + p
            own = owners[:, p * OBLK : (p + 1) * OBLK]
            col = (own & 7) * 1024 + slots[:, p * OBLK : (p + 1) * OBLK]
            mine = (own >> 3) == var
            tile = jnp.broadcast_to(jnp.where(mine, col >> 7, -64), (8, LANE))
            lane = jnp.broadcast_to(col & 127, (8, LANE))
            low = jnp.zeros((8, LANE), F32)
            for j in range(64):
                got = jnp.take_along_axis(
                    pay[:, j * LANE : (j + 1) * LANE], lane, axis=1, mode="promise_in_bounds"
                )
                low = jnp.where(tile == j, got, low)
            rest = jnp.zeros((8, LANE), F32)
            shifted = tile - quarter * 16
            for j in range(16):
                got = jnp.take_along_axis(
                    pay[:, WIDTH + j * LANE : WIDTH + (j + 1) * LANE], lane, axis=1, mode="promise_in_bounds"
                )
                rest = jnp.where(shifted == j, got, rest)
            block = jnp.where(mine, col >> 8, LANE - 1)
            local = jnp.take_along_axis(
                weights, jnp.broadcast_to(block, (8, LANE)), axis=1, mode="promise_in_bounds"
            )
            c, y = g // 8, g % 8
            base = (y * NX * NC + c) * 3
            high = [
                jnp.sum(jnp.where((row & 1) == m, rest, 0.0), axis=0, keepdims=True) for m in range(2)
            ]
            out[base : base + 3] = low[0:3]
            out[base + 3 * NC : base + 3 * NC + 3] = low[3:6]
            out[base + 6 * NC : base + 6 * NC + 2] = low[6:8]
            out[base + 6 * NC + 2 : base + 6 * NC + 3] = high[0]
            out[base + 9 * NC : base + 9 * NC + 1] = high[1]
            out[base + 9 * NC + 1 : base + 9 * NC + 3] = local[0:2]


def chain_kernel(
    order, own_half, other_half, value, errvar, pattern, weight, out, obs, local, t3, tv, table,
):
    z = lax.axis_index("z")
    first_core = lax.axis_index("c") == 0

    for g in range(GROUPS):
        c, y = g // 8, g % 8
        cols = slice(g * LANE, (g + 1) * LANE)
        for m in range(MZ + 2):
            at = (m // 3) * NZ * NY * 3 + y * 3 + m % 3
            a = own_half[pl.ds(at, NZ, stride=NY * 3), :]
            b = other_half[pl.ds(at, NZ, stride=NY * 3), :]
            row = jnp.where(first_core, a, b) if c == 0 else jnp.where(first_core, b, a)
            if m < MZ:
                obs[m * 8 : m * 8 + 8, cols] = row
            else:
                local[(m - MZ) * 8 : (m - MZ) * 8 + 8, cols] = row

    table[...] = jnp.zeros_like(table)
    for s in range(NB):
        names, sizes = pattern[order[s]], weight[order[s]]
        for p in range(4):
            hit = jnp.where(names == p, sizes, 0.0)
            table[4 * s + p : 4 * s + p + 1, 0:NBLK] = jnp.sum(hit, axis=0, keepdims=True)
    by_block = jnp.transpose(table[...])

    lanes = lax.broadcasted_iota(jnp.int32, (M, K3), 1)
    for t in range(NB):
        batch = order[t]
        val = value[pl.ds(batch, 1), :]
        err = errvar[pl.ds(batch, 1), :]
        prior = obs[:, t * NOBS : (t + 1) * NOBS]
        center = jnp.sum(prior, axis=0, keepdims=True) * (1.0 / M)
        pert = prior - center
        spread = jnp.sum(pert * pert, axis=0, keepdims=True) * (1.0 / (M - 1))
        total = spread + err
        posterior = (center * err + val * spread) / total
        factor = jnp.sqrt(err / total)
        increment = (posterior - center) + (factor - 1.0) * pert
        gain = pert * (1.0 / ((M - 1) * (spread + 1e-6)))
        gain = gain - jnp.sum(gain, axis=0, keepdims=True) * (1.0 / M)
        ih, il = halves(increment)
        gh, gl = halves(gain)
        for p in range(4):
            s = slice(p * OBLK, (p + 1) * OBLK)
            left = jnp.concatenate([ih[:, s], ih[:, s], il[:, s]], axis=1)
            right = jnp.concatenate([gh[:, s], gl[:, s], gh[:, s]], axis=1)
            right = jnp.concatenate([right, right, right], axis=0)
            mix = lax.dot_general(left, right, (((1,), (1,)), ((), ())), preferred_element_type=F32)
            t3[p * M : (p + 1) * M, :] = high_high_low(mix, lanes).astype(BF16)
            mh, ml = halves(mix)
            tv[4 * t + p] = jnp.concatenate([mh, ml, mh], axis=0)
        if t < NB - 1:
            mixing = t3[...]
            for n in range((t + 1) * NOBS, NB * NOBS, 256):
                x = obs[:, n : n + 256]
                xh, xl = halves(x)
                got = jnp.dot(mixing, jnp.concatenate([xh, xl, xh], axis=0), preferred_element_type=F32)
                for p in range(4):
                    row = (p % 2) * 8 + 2 * t + p // 2
                    x = x + local[row : row + 1, n : n + 256] * got[p * M : (p + 1) * M]
                obs[:, n : n + 256] = x

    rows = MZ * NBLK
    lane = lax.broadcasted_iota(jnp.int32, (rows, K3), 1)
    within = lane - jnp.where(lane >= 2 * M, 2 * M, jnp.where(lane >= M, M, 0))
    member = lax.broadcasted_iota(jnp.int32, (rows, K3), 0) // NBLK
    unit = (within == member * NZ + z).astype(F32)
    delta = jnp.zeros((rows, K3), F32)
    for s in reversed(range(NB)):
        left = high_high_low(unit + delta, lane).astype(BF16)
        for p in range(4):
            got = jnp.dot(left, tv[4 * s + p], preferred_element_type=F32)
            w = jnp.broadcast_to(by_block[0:NBLK, 4 * s + p : 4 * s + p + 1], (NBLK, K3))
            delta = delta + jnp.concatenate([w] * MZ, axis=0) * got
    to = lax.broadcasted_iota(jnp.int32, (K3, K3), 1)
    third = jnp.where(to >= 2 * M, 2 * M, jnp.where(to >= M, M, 0))
    spot = to - third
    tail = spot - 64
    low = (spot & 7) * 8 + ((z + (spot >> 3)) & 7)
    high = 64 + (tail & 1) * 8 + ((z + (tail >> 1)) & 7)
    source = jnp.where(spot < 64, low, high)
    source = third + source
    swap = (lax.broadcasted_iota(jnp.int32, (K3, K3), 0) == source).astype(BF16)
    delta = high_high_low(delta, lane).astype(BF16)
    delta = jnp.dot(delta, swap, preferred_element_type=F32)
    out[0] = delta[:, 0:LANE]
    out[1, :, 0 : K3 - LANE] = delta[:, LANE:K3]
    out[1, :, K3 - LANE : LANE] = jnp.zeros((rows, 2 * LANE - K3), F32)


def apply_kernel(delta, ens, s0, s1, s2, s3, s4, s5, s6, s7, out, tails):
    states = [s0, s1, s2, s3, s4, s5, s6, s7]
    for q in range(4):
        for i in range(NZ):
            tails[q, 2 * i : 2 * i + 2, :] = states[i][2 * q : 2 * q + 2, WIDTH:]
    for b in range(NBLK):
        cols = slice(b * VBLK, (b + 1) * VBLK)
        q, r = b // 8, b % 8
        x = [state[:, cols] for state in states] + [tails[q, :, r * VBLK : (r + 1) * VBLK]]
        xh, xl = halves(jnp.concatenate(x, axis=0))
        left = [delta[i, pl.ds(b, MZ, stride=NBLK), :] for i in range(2)]
        left = jnp.concatenate(left, axis=1)[:, 0:K3].astype(BF16)
        got = jnp.dot(left, jnp.concatenate([xh, xl, xh], axis=0), preferred_element_type=F32)
        out[:, cols] = ens[:, cols] + got


def per_device(ensemble, owner, slot, pattern, loc_weight, obs_value, obs_errvar, batch_order):
    vmem = pl.BlockSpec(memory_space=pltpu.VMEM)
    smem = pl.BlockSpec(memory_space=pltpu.SMEM)
    names = jnp.transpose(pattern, (0, 2, 1))
    sizes = jnp.transpose(loc_weight, (0, 2, 1))
    placed, pay = pl.pallas_call(
        extract_kernel,
        out_shape=[
            jax.ShapeDtypeStruct((NY * NX * NC * 3, LANE), F32),
            jax.ShapeDtypeStruct((8, 10240), F32),
        ],
        in_specs=[smem, vmem, vmem, vmem, vmem, vmem],
        out_specs=[vmem, vmem],
        scratch_shapes=[pltpu.VMEM((8, LANE), F32)],
    )(batch_order, ensemble, jnp.transpose(owner, (0, 2, 1)), slot, names, sizes)
    up = [(i, (i + 1) % NZ) for i in range(NZ)]
    down = [(i, (i - 1) % NZ) for i in range(NZ)]

    s7, s1 = lax.ppermute(pay, "z", up), lax.ppermute(pay, "z", down)
    placed = placed.reshape(NY * NX * NC, 1, 3 * LANE)
    parts = lax.all_to_all(placed, ("y", "x", "c"), split_axis=0, concat_axis=0, tiled=True)
    s6, s2 = lax.ppermute(s7, "z", up), lax.ppermute(s1, "z", down)
    mine = jnp.sum(parts, axis=0, keepdims=True)
    mine = jnp.broadcast_to(mine, (NZ * NY, 1, 3 * LANE))
    plane = lax.all_to_all(mine, ("z", "y"), split_axis=0, concat_axis=0, tiled=True)
    s5, s3 = lax.ppermute(s6, "z", up), lax.ppermute(s2, "z", down)
    plane = jnp.broadcast_to(plane.reshape(1, NZ * NY * 3, LANE), (NX, NZ * NY * 3, LANE))
    half = lax.all_to_all(plane, "x", split_axis=0, concat_axis=0, tiled=True)
    s4 = lax.ppermute(s3, "z", down)
    half = half.reshape(NX * NZ * NY * 3, LANE)
    other = lax.ppermute(half, "c", [(0, 1), (1, 0)])
    delta = pl.pallas_call(
        chain_kernel,
        out_shape=jax.ShapeDtypeStruct((2, MZ * NBLK, LANE), F32),
        in_specs=[smem] + [vmem] * 6,
        out_specs=vmem,
        scratch_shapes=[
            pltpu.VMEM((M, NB * NOBS), F32),
            pltpu.VMEM((16, NB * NOBS), F32),
            pltpu.VMEM((4 * M, K3), BF16),
            pltpu.VMEM((16, K3, K3), BF16),
            pltpu.VMEM((LANE, LANE), F32),
        ],
        compiler_params=pltpu.CompilerParams(vmem_limit_bytes=32 << 20),
    )(batch_order, half, other, obs_value, obs_errvar, names, sizes)
    return pl.pallas_call(
        apply_kernel,
        out_shape=jax.ShapeDtypeStruct((MZ, WIDTH), F32),
        in_specs=[vmem] * 10,
        out_specs=vmem,
        scratch_shapes=[pltpu.VMEM((4, 16, WIDTH // 4), F32)],
        compiler_params=pltpu.CompilerParams(vmem_limit_bytes=32 << 20),
    )(delta, ensemble, pay, s1, s2, s3, s4, s5, s6, s7)


def solution(mesh):
    fine = Mesh(mesh.devices.reshape(NZ, NY, NX, NC), ("z", "y", "x", "c"))
    var = ("y", "x", "c")
    in_specs = (P("z", var), P(), P(), P(None, var, None), P(None, var, None), P(), P(), P())
    return jax.shard_map(
        per_device, mesh=fine, in_specs=in_specs, out_specs=P("z", var), check_vma=False
    )
```

```python
import jax
import jax.numpy as jnp
from jax import lax
from jax.experimental import pallas as pl
from jax.experimental.pallas import tpu as pltpu
from jax.sharding import Mesh, PartitionSpec as P

M, NOBS, NB = 80, 512, 4
NZ, NY, NX, NC = 8, 8, 4, 2
MZ = M // NZ
WIDTH = 8192
VBLK = 256
NBLK = WIDTH // VBLK
OBLK = 128
GROUPS = NB * NOBS // OBLK
LANE = 128
K3 = 3 * M
F32, BF16 = jnp.float32, jnp.bfloat16


def halves(x):
    high = x.astype(BF16)
    return high, (x - high.astype(F32)).astype(BF16)


def high_high_low(x, lanes):
    high = x.astype(BF16).astype(F32)
    return jnp.where(lanes < 2 * M, high, x - high)


def extract_kernel(order, ens, owner, slot, pattern, weight, out, pay, table):
    z = lax.axis_index("z")
    var = (lax.axis_index("y") * NX + lax.axis_index("x")) * NC + lax.axis_index("c")
    pay[:, 0:WIDTH] = ens[0:8, :]
    for m in range(2):
        for quarter in range(4):
            row = 2 * quarter + m
            at = quarter * (WIDTH // 4)
            pay[row : row + 1, WIDTH:] = ens[8 + m : 9 + m, at : at + WIDTH // 4]
    q = order[z // 2]
    first = (z % 2) * 2
    table[...] = jnp.zeros_like(table)
    names, sizes = pattern[q], weight[q]
    for j in range(2):
        hit = jnp.where(names == first + j, sizes, 0.0)
        table[j : j + 1, 0:NBLK] = jnp.sum(hit, axis=0, keepdims=True)
    weights = table[...]
    row = lax.broadcasted_iota(jnp.int32, (8, LANE), 0)
    quarter = row >> 1
    for t in range(NB):
        batch = order[t]
        owners = owner[batch]
        slots = slot[pl.ds(batch, 1), :]
        for p in range(4):
            g = 4 * t + p
            own = owners[:, p * OBLK : (p + 1) * OBLK]
            col = (own & 7) * 1024 + slots[:, p * OBLK : (p + 1) * OBLK]
            mine = (own >> 3) == var
            tile = jnp.broadcast_to(jnp.where(mine, col >> 7, -64), (8, LANE))
            lane = jnp.broadcast_to(col & 127, (8, LANE))
            low = jnp.zeros((8, LANE), F32)
            for j in range(64):
                got = jnp.take_along_axis(
                    pay[:, j * LANE : (j + 1) * LANE], lane, axis=1, mode="promise_in_bounds"
                )
                low = jnp.where(tile == j, got, low)
            rest = jnp.zeros((8, LANE), F32)
            shifted = tile - quarter * 16
            for j in range(16):
                got = jnp.take_along_axis(
                    pay[:, WIDTH + j * LANE : WIDTH + (j + 1) * LANE], lane, axis=1, mode="promise_in_bounds"
                )
                rest = jnp.where(shifted == j, got, rest)
            block = jnp.where(mine, col >> 8, LANE - 1)
            local = jnp.take_along_axis(
                weights, jnp.broadcast_to(block, (8, LANE)), axis=1, mode="promise_in_bounds"
            )
            c, y = g // 8, g % 8
            base = (y * NX * NC + c) * 3
            high = [
                jnp.sum(jnp.where((row & 1) == m, rest, 0.0), axis=0, keepdims=True) for m in range(2)
            ]
            out[base : base + 3] = low[0:3]
            out[base + 3 * NC : base + 3 * NC + 3] = low[3:6]
            out[base + 6 * NC : base + 6 * NC + 2] = low[6:8]
            out[base + 6 * NC + 2 : base + 6 * NC + 3] = high[0]
            out[base + 9 * NC : base + 9 * NC + 1] = high[1]
            out[base + 9 * NC + 1 : base + 9 * NC + 3] = local[0:2]


def chain_kernel(
    order, own_half, other_half, value, errvar, pattern, weight, out, obs, local, t3, tv, table,
):
    z = lax.axis_index("z")
    first_core = lax.axis_index("c") == 0

    def place(source, c):
        for y in range(NY):
            g = c * NY + y
            cols = slice(g * LANE, (g + 1) * LANE)
            for m in range(MZ + 2):
                at = (m // 3) * NZ * NY * 3 + y * 3 + m % 3
                row = source[pl.ds(at, NZ, stride=NY * 3), :]
                if m < MZ:
                    obs[m * 8 : m * 8 + 8, cols] = row
                else:
                    local[(m - MZ) * 8 : (m - MZ) * 8 + 8, cols] = row

    @pl.when(first_core)
    def _():
        place(own_half, 0)
        place(other_half, 1)

    @pl.when(jnp.logical_not(first_core))
    def _():
        place(other_half, 0)
        place(own_half, 1)

    table[...] = jnp.zeros_like(table)
    for s in range(NB):
        names, sizes = pattern[order[s]], weight[order[s]]
        for p in range(4):
            hit = jnp.where(names == p, sizes, 0.0)
            table[4 * s + p : 4 * s + p + 1, 0:NBLK] = jnp.sum(hit, axis=0, keepdims=True)
    by_block = jnp.transpose(table[...])

    lanes = lax.broadcasted_iota(jnp.int32, (M, K3), 1)
    for t in range(NB):
        batch = order[t]
        val = value[pl.ds(batch, 1), :]
        err = errvar[pl.ds(batch, 1), :]
        prior = obs[:, t * NOBS : (t + 1) * NOBS]
        center = jnp.sum(prior, axis=0, keepdims=True) * (1.0 / M)
        pert = prior - center
        spread = jnp.sum(pert * pert, axis=0, keepdims=True) * (1.0 / (M - 1))
        total = spread + err
        posterior = (center * err + val * spread) / total
        factor = jnp.sqrt(err / total)
        increment = (posterior - center) + (factor - 1.0) * pert
        gain = pert * (1.0 / ((M - 1) * (spread + 1e-6)))
        gain = gain - jnp.sum(gain, axis=0, keepdims=True) * (1.0 / M)
        ih, il = halves(increment)
        gh, gl = halves(gain)
        for p in range(4):
            s = slice(p * OBLK, (p + 1) * OBLK)
            left = jnp.concatenate([ih[:, s], ih[:, s], il[:, s]], axis=1)
            right = jnp.concatenate([gh[:, s], gl[:, s], gh[:, s]], axis=1)
            right = jnp.concatenate([right, right, right], axis=0)
            mix = lax.dot_general(left, right, (((1,), (1,)), ((), ())), preferred_element_type=F32)
            t3[p * M : (p + 1) * M, :] = high_high_low(mix, lanes).astype(BF16)
            mh, ml = halves(mix)
            tv[4 * t + p] = jnp.concatenate([mh, ml, mh], axis=0)
        if t < NB - 1:
            mixing = t3[...]
            for n in range((t + 1) * NOBS, NB * NOBS, 256):
                x = obs[:, n : n + 256]
                xh, xl = halves(x)
                got = jnp.dot(mixing, jnp.concatenate([xh, xl, xh], axis=0), preferred_element_type=F32)
                for p in range(4):
                    row = (p % 2) * 8 + 2 * t + p // 2
                    x = x + local[row : row + 1, n : n + 256] * got[p * M : (p + 1) * M]
                obs[:, n : n + 256] = x

    rows = MZ * NBLK
    lane = lax.broadcasted_iota(jnp.int32, (rows, K3), 1)
    within = lane - jnp.where(lane >= 2 * M, 2 * M, jnp.where(lane >= M, M, 0))
    member = lax.broadcasted_iota(jnp.int32, (rows, K3), 0) // NBLK
    unit = (within == member * NZ + z).astype(F32)
    delta = jnp.zeros((rows, K3), F32)
    for s in reversed(range(NB)):
        left = high_high_low(unit + delta, lane).astype(BF16)
        for p in range(4):
            got = jnp.dot(left, tv[4 * s + p], preferred_element_type=F32)
            w = jnp.broadcast_to(by_block[0:NBLK, 4 * s + p : 4 * s + p + 1], (NBLK, K3))
            delta = delta + jnp.concatenate([w] * MZ, axis=0) * got
    to = lax.broadcasted_iota(jnp.int32, (K3, K3), 1)
    third = jnp.where(to >= 2 * M, 2 * M, jnp.where(to >= M, M, 0))
    spot = to - third
    tail = spot - 64
    low = (spot & 7) * 8 + ((z + (spot >> 3)) & 7)
    high = 64 + (tail & 1) * 8 + ((z + (tail >> 1)) & 7)
    source = jnp.where(spot < 64, low, high)
    source = third + source
    swap = (lax.broadcasted_iota(jnp.int32, (K3, K3), 0) == source).astype(BF16)
    delta = high_high_low(delta, lane).astype(BF16)
    delta = jnp.dot(delta, swap, preferred_element_type=F32)
    out[0] = delta[:, 0:LANE]
    out[1, :, 0 : K3 - LANE] = delta[:, LANE:K3]
    out[1, :, K3 - LANE : LANE] = jnp.zeros((rows, 2 * LANE - K3), F32)


def apply_kernel(delta, ens, s0, s1, s2, s3, s4, s5, s6, s7, out, tails):
    states = [s0, s1, s2, s3, s4, s5, s6, s7]
    for q in range(4):
        for i in range(NZ):
            tails[q, 2 * i : 2 * i + 2, :] = states[i][2 * q : 2 * q + 2, WIDTH:]
    for b in range(NBLK):
        cols = slice(b * VBLK, (b + 1) * VBLK)
        q, r = b // 8, b % 8
        x = [state[:, cols] for state in states] + [tails[q, :, r * VBLK : (r + 1) * VBLK]]
        xh, xl = halves(jnp.concatenate(x, axis=0))
        left = [delta[i, pl.ds(b, MZ, stride=NBLK), :] for i in range(2)]
        left = jnp.concatenate(left, axis=1)[:, 0:K3].astype(BF16)
        got = jnp.dot(left, jnp.concatenate([xh, xl, xh], axis=0), preferred_element_type=F32)
        out[:, cols] = ens[:, cols] + got


def per_device(ensemble, owner, slot, pattern, loc_weight, obs_value, obs_errvar, batch_order):
    vmem = pl.BlockSpec(memory_space=pltpu.VMEM)
    smem = pl.BlockSpec(memory_space=pltpu.SMEM)
    names = jnp.transpose(pattern, (0, 2, 1))
    sizes = jnp.transpose(loc_weight, (0, 2, 1))
    placed, pay = pl.pallas_call(
        extract_kernel,
        out_shape=[
            jax.ShapeDtypeStruct((NY * NX * NC * 3, LANE), F32),
            jax.ShapeDtypeStruct((8, 10240), F32),
        ],
        in_specs=[smem, vmem, vmem, vmem, vmem, vmem],
        out_specs=[vmem, vmem],
        scratch_shapes=[pltpu.VMEM((8, LANE), F32)],
    )(batch_order, ensemble, jnp.transpose(owner, (0, 2, 1)), slot, names, sizes)
    up = [(i, (i + 1) % NZ) for i in range(NZ)]
    down = [(i, (i - 1) % NZ) for i in range(NZ)]

    s7, s1 = lax.ppermute(pay, "z", up), lax.ppermute(pay, "z", down)
    placed = placed.reshape(NY * NX * NC, 1, 3 * LANE)
    parts = lax.all_to_all(placed, ("y", "x", "c"), split_axis=0, concat_axis=0, tiled=True)
    s6, s2 = lax.ppermute(s7, "z", up), lax.ppermute(s1, "z", down)
    mine = jnp.sum(parts, axis=0, keepdims=True)
    mine = jnp.broadcast_to(mine, (NZ * NY, 1, 3 * LANE))
    plane = lax.all_to_all(mine, ("z", "y"), split_axis=0, concat_axis=0, tiled=True)
    s5, s3 = lax.ppermute(s6, "z", up), lax.ppermute(s2, "z", down)
    plane, _ = lax.optimization_barrier((plane, s2))
    plane = jnp.broadcast_to(plane.reshape(1, NZ * NY * 3, LANE), (NX, NZ * NY * 3, LANE))
    half = lax.all_to_all(plane, "x", split_axis=0, concat_axis=0, tiled=True)
    s4 = lax.ppermute(s3, "z", down)
    half = half.reshape(NX * NZ * NY * 3, LANE)
    other = lax.ppermute(half, "c", [(0, 1), (1, 0)])
    delta = pl.pallas_call(
        chain_kernel,
        out_shape=jax.ShapeDtypeStruct((2, MZ * NBLK, LANE), F32),
        in_specs=[smem] + [vmem] * 6,
        out_specs=vmem,
        scratch_shapes=[
            pltpu.VMEM((M, NB * NOBS), F32),
            pltpu.VMEM((16, NB * NOBS), F32),
            pltpu.VMEM((4 * M, K3), BF16),
            pltpu.VMEM((16, K3, K3), BF16),
            pltpu.VMEM((LANE, LANE), F32),
        ],
        compiler_params=pltpu.CompilerParams(vmem_limit_bytes=32 << 20),
    )(batch_order, half, other, obs_value, obs_errvar, names, sizes)
    return pl.pallas_call(
        apply_kernel,
        out_shape=jax.ShapeDtypeStruct((MZ, WIDTH), F32),
        in_specs=[vmem] * 10,
        out_specs=vmem,
        scratch_shapes=[pltpu.VMEM((4, 16, WIDTH // 4), F32)],
        compiler_params=pltpu.CompilerParams(vmem_limit_bytes=32 << 20),
    )(delta, ensemble, pay, s1, s2, s3, s4, s5, s6, s7)


def solution(mesh):
    fine = Mesh(mesh.devices.reshape(NZ, NY, NX, NC), ("z", "y", "x", "c"))
    var = ("y", "x", "c")
    in_specs = (P("z", var), P(), P(), P(None, var, None), P(None, var, None), P(), P(), P())
    return jax.shard_map(
        per_device, mesh=fine, in_specs=in_specs, out_specs=P("z", var), check_vma=False
    )
```
